32 devices in a mesh: donor: 16 (over z, y, x), gene: 2 (over core).
Axes of the slice: x: 2, y: 2, z: 4, core: 2. Of those that a mesh axis runs over, the one named last changes fastest.
Arguments:
- embeddings: bfloat16 [32768, 512], P('donor', 'gene')
- targets_by_gene: bfloat16 [5120, 32768], P(('gene', 'donor')), may hold values from -6 to 6
- cell_counts: int32 [16], P('donor'), may hold values from 1024 to 2048, as said below
Outputs:
- coefficients: float32 [512, 5120], P('donor', 'gene')
The draws below stay inside these ranges and needn't reach their ends.
Inputs may be any that keep to these rules, and one draw needn't show every extreme that they name: `cell_counts`: every entry is a multiple of 128; some entry equals 2048 and some entry equals 2048/2.
All inputs are finite; a program needn't handle non-finite values.
Results may differ from the reference program's by a relative error of at most 0.0003.
Values may be sent and summed in bfloat16 or wider, within the bound.
No kernel may reach another device: no remote copies, remote signals or barrier semaphores. Data moves between devices by JAX's collectives and lax.ppermute only.
A program may use at most 128 MiB of HBM per device.

```python
import math
import jax
import jax.numpy as jnp
from jax import lax

D = 512
GENES = 5120
ROWS_DEV = 2048
TILE = 128
CELLS = 32768
N_DONOR = 16


def draw_embeddings(key, part):
    key_noise, key_cols, key_rows = jax.random.split(jax.random.fold_in(key, 11), 3)
    noise = jax.random.normal(key_noise, (CELLS, D), jnp.float32)
    col_scale = jnp.exp(jax.random.uniform(key_cols, (1, D), jnp.float32, -1.1512925, 1.1512925))
    row_scale = jnp.exp(jax.random.uniform(key_rows, (CELLS, 1), jnp.float32, -1.1512925, 1.1512925))
    values = noise * col_scale * row_scale
    return values.astype(jnp.bfloat16)


def draw_cell_counts(key, part):
    key_tiles, key_order = jax.random.split(jax.random.fold_in(key, 23), 2)
    low_tiles = ROWS_DEV // (2 * TILE)
    high_tiles = ROWS_DEV // TILE
    tiles = jax.random.randint(key_tiles, (N_DONOR,), low_tiles, high_tiles + 1, dtype=jnp.int32)
    order = jax.random.permutation(key_order, N_DONOR)
    tiles = tiles.at[order[0]].set(high_tiles)
    tiles = tiles.at[order[1]].set(low_tiles)
    return (tiles * TILE).astype(jnp.int32)


def level_of(own_key, extent, pieces, low, largest):
    def one(dim, parts):
        heights = jax.random.uniform(jax.random.fold_in(jax.random.fold_in(own_key, 6), dim), (parts,), jnp.float32, low / len(pieces), largest / len(pieces))
        return jnp.repeat(jnp.exp(heights), extent[dim] // parts).reshape((-1,) + (1,) * (len(extent) - dim - 1))

    factor_of = one(*pieces[0])
    for cut in pieces[1:]:
        factor_of = factor_of * one(*cut)
    return factor_of


def normal_values(rng, dims, spread, most, cuts=(), kind=jnp.bfloat16):
    array = jax.random.normal(rng, dims, jnp.float32) * spread
    if len(cuts) > 0:
        array = level_of(rng, dims, cuts, -0.22, 0.18) * array
    return jnp.clip(array, min=-most, max=most).astype(kind)


def setup_inputs(seed: int = 0) -> dict:
    streams_of = jax.random.split(jax.random.key(seed), 4)
    return {
        "embeddings": draw_embeddings(jax.random.fold_in(streams_of[3], 71), 0),
        "targets_by_gene": normal_values(streams_of[1], (GENES, CELLS), 1.0, 6.0, ((0, 32),)),
        "cell_counts": draw_cell_counts(jax.random.fold_in(streams_of[3], 71), 0),
    }


def reference(embeddings, targets_by_gene, cell_counts):
    row_index = jnp.arange(CELLS, dtype=jnp.int32)
    owner = row_index // ROWS_DEV
    within = row_index % ROWS_DEV
    row_valid = within < cell_counts[owner]
    masked = jnp.where(row_valid[:, None], embeddings, jnp.zeros_like(embeddings))
    masked_wide = masked.astype(jnp.float32)
    block_genes = 128
    gene_blocks = targets_by_gene.reshape(GENES // block_genes, block_genes, CELLS)

    def one_block(block):
        return jnp.dot(block.astype(jnp.float32), masked_wide, precision=lax.Precision.HIGHEST)
    cross = lax.map(one_block, gene_blocks).reshape(GENES, D)
    factor = jnp.linalg.qr(masked_wide, mode='r')
    halfway = lax.linalg.triangular_solve(factor, cross.T, left_side=True, lower=False, transpose_a=True)
    solution = lax.linalg.triangular_solve(factor, halfway, left_side=True, lower=False)
    return (math.sqrt(CELLS) * solution).astype(jnp.float32)
```

```python
import functools
import math

import jax
import jax.numpy as jnp
from jax import lax
from jax.experimental import pallas as pl
from jax.experimental.pallas import tpu as pltpu
from jax.sharding import PartitionSpec as P

AXES = ("donor", "gene")
HI = lax.Precision.HIGHEST
VMEM_BYTES = 48 * 1024 * 1024


def solve_both(lower_factor, right_cols):
    halfway = lax.linalg.triangular_solve(lower_factor, right_cols, left_side=True, lower=True)
    return lax.linalg.triangular_solve(
        lower_factor, halfway, left_side=True, lower=True, transpose_a=True
    )


def shards_any_mesh(embeddings, targets_by_gene, cell_counts):
    valid_count = cell_counts[0]
    gathered = lax.all_gather(embeddings, "gene", axis=1, tiled=True)
    row_total = gathered.shape[0]
    width = gathered.shape[1]
    donors = lax.axis_size("donor")
    row_valid = lax.broadcasted_iota(jnp.int32, (row_total, 1), 0) < valid_count
    masked = jnp.where(row_valid, gathered, jnp.zeros_like(gathered))
    gram_matrix = lax.dot_general(
        masked, masked, (((0,), (0,)), ((), ())), preferred_element_type=jnp.float32
    )
    by_rows = lax.all_to_all(targets_by_gene, "donor", split_axis=1, concat_axis=0, tiled=True)
    gram_matrix = lax.psum(gram_matrix, "donor")
    lower_factor = jnp.linalg.cholesky(gram_matrix)
    scale_total = math.sqrt(row_total * donors)
    cross_local = jnp.dot(by_rows, masked, preferred_element_type=jnp.float32)
    cross_sum = lax.psum(cross_local, "donor")
    scaled = scale_total * solve_both(lower_factor, cross_sum.T)
    share = width // donors
    first_row = lax.axis_index("donor") * share
    return lax.dynamic_slice_in_dim(scaled, first_row, share, 0)


def permutation(target):
    pairs = []
    for z in range(4):
        for y in range(2):
            for x in range(2):
                for c in range(2):
                    there = target(z, y, x, c)
                    if there is not None:
                        tz, ty, tx, tc = there
                        pairs.append((((z * 2 + y) * 2 + x) * 2 + c, ((tz * 2 + ty) * 2 + tx) * 2 + tc))
    return pairs


CORE = permutation(lambda z, y, x, c: (z, y, x, 1 - c))
NEAR = permutation(lambda z, y, x, c: (z, y, 1 - x, c) if c == 0 else (z, 1 - y, x, c))
FAR = permutation(lambda z, y, x, c: (z, 1 - y, x, c) if c == 0 else (z, y, 1 - x, c))
DIAG_OUT = permutation(lambda z, y, x, c: (z, 1 - y, x, 1) if c == 0 else (z, y, 1 - x, 0))
DIAG_BACK = permutation(lambda z, y, x, c: (z, y, 1 - x, 1) if c == 0 else (z, 1 - y, x, 0))
UP = permutation(lambda z, y, x, c: (z + 1, y, x, c) if z < 3 else None)
DOWN = permutation(lambda z, y, x, c: (z - 1, y, x, c) if z > 0 else None)
ZXOR = [permutation(lambda z, y, x, c, s=s: (z ^ s, y, x, c)) for s in (1, 2, 3)]


def send(value, perm):
    return lax.ppermute(value, AXES, perm)


def pick_kernel(index_ref, t_ref, o_ref):
    o_ref[0] = t_ref[...]


def pick_blocks(targets, block_index, block_cells):
    rows = targets.shape[0]
    count = block_index.shape[0]
    return pl.pallas_call(
        pick_kernel,
        out_shape=jax.ShapeDtypeStruct((count, rows, block_cells), targets.dtype),
        grid_spec=pltpu.PrefetchScalarGridSpec(
            num_scalar_prefetch=1,
            grid=(count,),
            in_specs=[pl.BlockSpec((rows, block_cells), lambda k, index: (0, index[k]))],
            out_specs=pl.BlockSpec((1, rows, block_cells), lambda k, index: (k, 0, 0)),
        ),
        cost_estimate=pl.CostEstimate(
            flops=0, bytes_accessed=4 * count * rows * block_cells, transcendentals=0
        ),
        name="pick_blocks",
    )(block_index, targets)


def cross_kernel(index_ref, own_ref, core_ref, near_ref, diag_ref, x_ref, *rest):
    prior_ref, o_ref = rest if len(rest) == 2 else (None, rest[0])
    rows = own_ref.shape[0]
    block = x_ref[...]
    for q, piece in enumerate((own_ref[...], core_ref[0], near_ref[0], diag_ref[0])):
        part = jnp.dot(piece, block, preferred_element_type=jnp.float32)
        place = pl.ds(q * rows, rows)
        if prior_ref is not None:
            part = part + prior_ref[place, :]
        o_ref[place, :] = part


def cross_add(prior, block_index, slot, targets, from_core, from_near, from_diag, block):
    rows = targets.shape[0]
    cells, width = block.shape
    index = jnp.stack([block_index, slot]).astype(jnp.int32)
    piece = pl.BlockSpec((1, rows, cells), lambda i, index: (index[1], 0, 0))
    whole = lambda shape: pl.BlockSpec(shape, lambda i, index: (0, 0))
    in_specs = [
        pl.BlockSpec((rows, cells), lambda i, index: (0, index[0])),
        piece,
        piece,
        piece,
        whole((cells, width)),
    ]
    operands = [index, targets, from_core, from_near, from_diag, block]
    aliases = {}
    if prior is not None:
        in_specs.append(whole((4 * rows, width)))
        operands.append(prior)
        aliases = {6: 0}
    return pl.pallas_call(
        cross_kernel,
        out_shape=jax.ShapeDtypeStruct((4 * rows, width), jnp.float32),
        grid_spec=pltpu.PrefetchScalarGridSpec(
            num_scalar_prefetch=1,
            grid=(1,),
            in_specs=in_specs,
            out_specs=whole((4 * rows, width)),
        ),
        input_output_aliases=aliases,
        compiler_params=pltpu.CompilerParams(vmem_limit_bytes=VMEM_BYTES),
        cost_estimate=pl.CostEstimate(
            flops=8 * rows * cells * width, bytes_accessed=8 * rows * cells + 2 * cells * width, transcendentals=0
        ),
        name="cross_add",
    )(*operands)


def halves(value, bit):
    half = value.shape[0] // 2
    keep = lax.dynamic_slice_in_dim(value, bit * half, half, 0)
    give = lax.dynamic_slice_in_dim(value, (1 - bit) * half, half, 0)
    return keep, give


def join(mine, other, bit):
    low = jnp.where(bit == 0, mine, other)
    high = jnp.where(bit == 0, other, mine)
    return jnp.concatenate([low, high], axis=0)


def sum_everywhere(value, z, c, near_bit, far_bit):
    for bit, perm in ((c, CORE), (near_bit, NEAR), (far_bit, FAR)):
        keep, give = halves(value, bit)
        value = keep + send(give, perm)
    quarter = value.shape[0] // 4
    part = lambda i: lax.dynamic_slice_in_dim(value, i * quarter, quarter, 0)
    total = part(z)
    for s in (1, 2, 3):
        total = total + send(part(z ^ s), ZXOR[s - 1])
    parts = jnp.zeros_like(value)
    parts = lax.dynamic_update_slice_in_dim(parts, total, z * quarter, 0)
    for s in (1, 2, 3):
        parts = lax.dynamic_update_slice_in_dim(parts, send(total, ZXOR[s - 1]), (z ^ s) * quarter, 0)
    value = parts
    for bit, perm in ((far_bit, FAR), (near_bit, NEAR), (c, CORE)):
        value = join(value, send(value, perm), bit)
    return value


def shards(embeddings, targets_by_gene, cell_counts):
    slots = embeddings.shape[0]
    donors = lax.axis_size("donor")
    donor = lax.axis_index("donor")
    c = lax.axis_index("gene")
    z, y, x = donor // 4, (donor // 2) % 2, donor % 2
    near_bit = jnp.where(c == 0, x, y)
    far_bit = jnp.where(c == 0, y, x)
    half = slots // 2

    row_valid = lax.broadcasted_iota(jnp.int32, (slots, 1), 0) < cell_counts[0]
    masked = jnp.where(row_valid, embeddings, jnp.zeros_like(embeddings))
    keep, give = halves(masked, c)
    got = send(give, CORE)
    block = jnp.concatenate(
        [jnp.where(c == 0, keep, got), jnp.where(c == 0, got, keep)], axis=1
    )

    def group_donor(k, core, bit):
        line, other = k // 2, k % 2
        return line * 4 + jnp.where(core == 0, other * 2 + bit, bit * 2 + other)

    ks = jnp.arange(8, dtype=jnp.int32)

    def blocks_for(core, bit):
        return (group_donor(ks, core, bit) * 2 + core).astype(jnp.int32)

    far_bit_there = jnp.where(c == 0, y, x)
    from_near = send(pick_blocks(targets_by_gene, blocks_for(c, 1 - near_bit), half), NEAR)
    from_diag = send(pick_blocks(targets_by_gene, blocks_for(1 - c, 1 - far_bit_there), half), DIAG_OUT)
    from_core = send(pick_blocks(targets_by_gene, blocks_for(1 - c, far_bit_there), half), CORE)

    up1 = send(block, UP)
    down1 = send(block, DOWN)
    up2 = send(up1, UP)
    down2 = send(down1, DOWN)
    up3 = send(up2, UP)
    down3 = send(down2, DOWN)
    near_z = jnp.where(z == 0, down1, up1)
    mid_z = jnp.where(z <= 1, down2, up2)
    last_z = jnp.where(z == 0, down3, jnp.where(z == 3, up3, down1))
    lines = (
        (block, z),
        (near_z, jnp.where(z == 0, 1, z - 1)),
        (mid_z, jnp.where(z <= 1, z + 2, z - 2)),
        (last_z, jnp.where(z == 0, 3, jnp.where(z == 3, 0, z + 1))),
    )
    pieces = [(value, line, far_bit) for value, line in lines]
    pieces += [(send(value, FAR), line, 1 - far_bit) for value, line in lines]

    gram_matrix = lax.dot_general(
        block, block, (((0,), (0,)), ((), ())), preferred_element_type=jnp.float32
    )
    gram_matrix = sum_everywhere(gram_matrix, z, c, near_bit, far_bit)
    lower_factor = jnp.linalg.cholesky(gram_matrix)
    width = gram_matrix.shape[0]
    lower_inverse = lax.linalg.triangular_solve(
        lower_factor, jnp.eye(width, dtype=jnp.float32), left_side=True, lower=True
    )

    acc = None
    for value, line, other in pieces:
        k = line * 2 + other
        acc = cross_add(
            acc, group_donor(k, c, near_bit) * 2 + c, k, targets_by_gene, from_core, from_near, from_diag, value
        )
    rows = targets_by_gene.shape[0]
    part = lambda q: acc[q * rows : (q + 1) * rows]
    cross = part(0) + send(part(1), CORE) + send(part(2), NEAR) + send(part(3), DIAG_BACK)

    dims = lambda a, b: (((a,), (b,)), ((), ()))
    halfway = lax.dot_general(lower_inverse, cross, dims(1, 1), precision=HI)
    scaled = math.sqrt(slots * donors) * lax.dot_general(lower_inverse, halfway, dims(0, 0), precision=HI)
    return lax.all_to_all(scaled, "donor", split_axis=0, concat_axis=1, tiled=True)


def solution(mesh):
    placed = (P("donor", "gene"), P(("gene", "donor"), None), P("donor"))
    tuned = mesh.shape["donor"] == 16 and mesh.shape["gene"] == 2
    return jax.shard_map(
        shards if tuned else shards_any_mesh,
        mesh=mesh,
        in_specs=placed,
        out_specs=P("donor", "gene"),
        check_vma=False,
    )
```

```python
import functools
import math

import jax
import jax.numpy as jnp
from jax import lax
from jax.experimental import pallas as pl
from jax.experimental.pallas import tpu as pltpu
from jax.sharding import PartitionSpec as P

AXES = ("donor", "gene")
HI = lax.Precision.HIGHEST
VMEM_BYTES = 48 * 1024 * 1024
FACTOR_BYTES = 1


def solve_both(lower_factor, right_cols):
    halfway = lax.linalg.triangular_solve(lower_factor, right_cols, left_side=True, lower=True)
    return lax.linalg.triangular_solve(
        lower_factor, halfway, left_side=True, lower=True, transpose_a=True
    )


def shards_any_mesh(embeddings, targets_by_gene, cell_counts):
    valid_count = cell_counts[0]
    gathered = lax.all_gather(embeddings, "gene", axis=1, tiled=True)
    row_total = gathered.shape[0]
    width = gathered.shape[1]
    donors = lax.axis_size("donor")
    row_valid = lax.broadcasted_iota(jnp.int32, (row_total, 1), 0) < valid_count
    masked = jnp.where(row_valid, gathered, jnp.zeros_like(gathered))
    gram_matrix = lax.dot_general(
        masked, masked, (((0,), (0,)), ((), ())), preferred_element_type=jnp.float32
    )
    by_rows = lax.all_to_all(targets_by_gene, "donor", split_axis=1, concat_axis=0, tiled=True)
    gram_matrix = lax.psum(gram_matrix, "donor")
    lower_factor = jnp.linalg.cholesky(gram_matrix)
    scale_total = math.sqrt(row_total * donors)
    cross_local = jnp.dot(by_rows, masked, preferred_element_type=jnp.float32)
    cross_sum = lax.psum(cross_local, "donor")
    scaled = scale_total * solve_both(lower_factor, cross_sum.T)
    share = width // donors
    first_row = lax.axis_index("donor") * share
    return lax.dynamic_slice_in_dim(scaled, first_row, share, 0)


def permutation(target):
    pairs = []
    for z in range(4):
        for y in range(2):
            for x in range(2):
                for c in range(2):
                    there = target(z, y, x, c)
                    if there is not None:
                        tz, ty, tx, tc = there
                        pairs.append((((z * 2 + y) * 2 + x) * 2 + c, ((tz * 2 + ty) * 2 + tx) * 2 + tc))
    return pairs


CORE = permutation(lambda z, y, x, c: (z, y, x, 1 - c))
NEAR = permutation(lambda z, y, x, c: (z, y, 1 - x, c) if c == 0 else (z, 1 - y, x, c))
FAR = permutation(lambda z, y, x, c: (z, 1 - y, x, c) if c == 0 else (z, y, 1 - x, c))
DIAG_OUT = permutation(lambda z, y, x, c: (z, 1 - y, x, 1) if c == 0 else (z, y, 1 - x, 0))
DIAG_BACK = permutation(lambda z, y, x, c: (z, y, 1 - x, 1) if c == 0 else (z, 1 - y, x, 0))
PLANE = [permutation(lambda z, y, x, c, s=s: (z, y ^ (s >> 1), x ^ (s & 1), c)) for s in (1, 2, 3)]
LINE = [permutation(lambda z, y, x, c, s=s: (z ^ s, y, x, c)) for s in (1, 2, 3)]

MIDDLE = permutation(lambda z, y, x, c: (3 - z, y, x, c) if z in (1, 2) else None)
OUTWARD = permutation(lambda z, y, x, c: (z ^ 1, y, x, c) if z in (1, 2) else None)


def send(value, perm):
    return lax.ppermute(value, AXES, perm)


def pick_kernel(first_row, index_ref, t_ref, *rest):
    o_ref, held, in_sems, out_sems = rest[-4:]
    count, rows, block_cells = held.shape
    copies = []
    for k in range(count):
        start = pl.multiple_of(index_ref[k] * block_cells, block_cells)
        copies.append(
            (
                pltpu.make_async_copy(t_ref.at[first_row : first_row + rows, pl.ds(start, block_cells)], held.at[k], in_sems.at[k]),
                pltpu.make_async_copy(held.at[k], o_ref.at[k], out_sems.at[k]),
            )
        )
    for inward, _ in copies:
        inward.start()
    for inward, outward in copies:
        inward.wait()
        outward.start()
    for _, outward in copies:
        outward.wait()


def pick_blocks(targets, block_index, block_cells, after=(), first_row=0, rows=None):
    rows = rows or targets.shape[0]
    count = block_index.shape[0]
    return pl.pallas_call(
        functools.partial(pick_kernel, first_row),
        out_shape=jax.ShapeDtypeStruct((count, rows, block_cells), targets.dtype),
        in_specs=[pl.BlockSpec(memory_space=pltpu.SMEM)]
        + [pl.BlockSpec(memory_space=pl.ANY)] * (1 + len(after)),
        out_specs=pl.BlockSpec(memory_space=pl.ANY),
        scratch_shapes=[
            pltpu.VMEM((count, rows, block_cells), targets.dtype),
            pltpu.SemaphoreType.DMA((count,)),
            pltpu.SemaphoreType.DMA((count,)),
        ],
        compiler_params=pltpu.CompilerParams(vmem_limit_bytes=VMEM_BYTES),
        cost_estimate=pl.CostEstimate(flops=1, bytes_accessed=1, transcendentals=0),
        name="pick_blocks",
    )(block_index, targets, *after)


def cross_kernel(has_prior, blocks, index_ref, *refs):
    outs = refs[-4:]
    prior = refs[6 * blocks : 6 * blocks + 4]
    rows = outs[0].shape[0]
    for q in range(4):
        for first in (0, rows // 2) if q == 2 else (0,):
            total = None
            for n in range(blocks):
                own, from_core, near_low, near_high, from_diag, x_ref = refs[6 * n : 6 * n + 6]
                piece = (own[...], from_core[0], near_high[0] if first else near_low[0], from_diag[0])[q]
                part = jnp.dot(piece, x_ref[...], preferred_element_type=jnp.float32)
                total = part if total is None else total + part
            place = pl.ds(first, total.shape[0])
            outs[q][place, :] = total + prior[q][place, :] if has_prior else total


def cross_add(prior, targets, received, blocks, after=()):
    rows = targets.shape[0]
    whole = lambda shape: pl.BlockSpec(shape, lambda i, index: (0, 0))
    index, operands, in_specs = [], [], []
    for n, (block, column, slot, part) in enumerate(blocks):
        cells, width = block.shape
        index += [column, slot]
        operands += [targets, *received, block]
        in_specs += [pl.BlockSpec((rows, cells), lambda i, index, n=n: (0, index[2 * n]))]
        in_specs += [
            pl.BlockSpec((1, value.shape[1], cells), lambda i, index, n=n, part=part: (index[2 * n + 1], 0, part))
            for value in received
        ]
        in_specs += [whole((cells, width))]
    sums = [whole((rows, width))] * 4
    aliases = {1 + len(operands) + q: q for q in range(4)} if prior else {}
    return pl.pallas_call(
        functools.partial(cross_kernel, prior is not None, len(blocks)),
        out_shape=[jax.ShapeDtypeStruct((rows, width), jnp.float32)] * 4,
        grid_spec=pltpu.PrefetchScalarGridSpec(
            num_scalar_prefetch=1,
            grid=(1,),
            in_specs=in_specs + (sums if prior else []) + [pl.BlockSpec(memory_space=pl.ANY)] * len(after),
            out_specs=sums,
        ),
        input_output_aliases=aliases,
        compiler_params=pltpu.CompilerParams(vmem_limit_bytes=VMEM_BYTES),
        cost_estimate=pl.CostEstimate(flops=1, bytes_accessed=1, transcendentals=0),
        name="cross_add",
    )(jnp.stack(index).astype(jnp.int32), *operands, *(prior or ()), *after)


TILE = 128
SUB = 8


def inverse_root(value):
    root = lax.rsqrt(value)
    return root * (1.5 - 0.5 * value * root * root)


def factor_tiles(tiles):
    lane = lax.broadcasted_iota(jnp.int32, (SUB, TILE), 1)
    sub = lax.broadcasted_iota(jnp.int32, (SUB, TILE), 0)
    wide = lambda value: jnp.broadcast_to(value, (SUB, TILE))
    count = len(tiles)
    for p in range(count):
        low = p * SUB
        rows = tiles[p]
        cols = [wide(rows[:, low + k : low + k + 1]) for k in range(SUB)]
        inside = (lane >= low) & (lane < low + SUB)
        rows = jnp.where(inside, jnp.where(lane - low == sub, 1.0, 0.0), rows)
        for k in range(SUB):
            root = inverse_root(wide(cols[k][k : k + 1, :]))
            scaled = cols[k] * root
            for j in range(k + 1, SUB):
                cols[j] = cols[j] - scaled * wide(scaled[j : j + 1, :])
            pivot_row = wide(rows[k : k + 1, :]) * root
            rows = jnp.where(sub == k, pivot_row, jnp.where(sub > k, rows - scaled * pivot_row, rows))
        tiles[p] = rows
        if p + 1 < count:
            right = jnp.where(lane >= low + SUB, rows, 0.0)
            change = lax.dot_general(
                right, rows, (((0,), (0,)), ((), ())), precision=HI, preferred_element_type=jnp.float32
            )
            for i in range(p + 1, count):
                tiles[i] = jnp.where(inside, 0.0, tiles[i]) - change[i * SUB : (i + 1) * SUB, :]
    return jnp.concatenate(tiles, axis=0)


def factor_kernel(step, count, v_ref, o_ref):
    here = slice(step * TILE, (step + 1) * TILE)
    o_ref[...] = v_ref[...]
    inverse = factor_tiles([v_ref[step * TILE + i * SUB : step * TILE + (i + 1) * SUB, here] for i in range(TILE // SUB)])
    down = lax.broadcasted_iota(jnp.int32, (TILE, TILE), 0)
    across = lax.broadcasted_iota(jnp.int32, (TILE, TILE), 1)
    inverse = jnp.where(down >= across, inverse, 0.0)
    o_ref[here, :] = jnp.dot(inverse, v_ref[here, :], precision=HI, preferred_element_type=jnp.float32)
    o_ref[here, here] = inverse
    if step + 1 < count:
        below = slice((step + 1) * TILE, count * TILE)
        o_ref[below, here] = jnp.zeros((TILE * (count - step - 1), TILE), jnp.float32)
        o_ref[below, :] = o_ref[below, :] - lax.dot_general(
            o_ref[here, below], o_ref[here, :], (((0,), (0,)), ((), ())), precision=HI, preferred_element_type=jnp.float32
        )


ANYWHERE = pl.BlockSpec(memory_space=pl.ANY)
SCALARS = pl.BlockSpec(memory_space=pltpu.SMEM)
VECTORS = pl.BlockSpec(memory_space=pltpu.VMEM)


def small_kernel(body, name, scalars, values, out_shape, after=(), moved=1):
    def kernel(*refs):
        given = len(scalars) + len(values)
        body(refs[:given], refs[given + len(after) :])

    return pl.pallas_call(
        kernel,
        out_shape=out_shape,
        in_specs=[SCALARS] * len(scalars) + [VECTORS] * len(values) + [ANYWHERE] * len(after),
        compiler_params=pltpu.CompilerParams(vmem_limit_bytes=VMEM_BYTES),
        cost_estimate=pl.CostEstimate(flops=1, bytes_accessed=moved, transcendentals=0),
        name=name,
    )(*scalars, *values, *after)


def f32(*shape):
    return jax.ShapeDtypeStruct(shape, jnp.float32)


def gram_rows(which, block, after=()):
    cells, width = block.shape
    half = width // 2

    def body(given, outs):
        which_ref, x_ref = given
        columns = x_ref[:, pl.ds(pl.multiple_of(which_ref[0] * half, half), half)]
        outs[0][...] = lax.dot_general(
            columns, x_ref[...], (((0,), (0,)), ((), ())), preferred_element_type=jnp.float32
        )

    return small_kernel(body, "gram_rows", [which], [block], f32(half, width), after)


def add_split(order, parts, after=()):
    rows, width = parts[0].shape
    count = order.shape[0]
    share = rows // count

    def body(given, outs):
        order_ref, part_refs = given[0], given[1:]
        for k in range(count):
            place = pl.ds(pl.multiple_of(order_ref[k] * share, share), share)
            total = part_refs[0][place, :]
            for ref in part_refs[1:]:
                total = total + ref[place, :]
            outs[k][...] = total

    return small_kernel(body, "add_split", [order], parts, [f32(share, width)] * count, after)


def add_all(parts, after=()):
    def body(given, outs):
        total = given[0][...]
        for ref in given[1:]:
            total = total + ref[...]
        outs[0][...] = total

    return small_kernel(body, "add_all", [], parts, f32(*parts[0].shape), after)


def place_parts(order, parts, after=()):
    share, width = parts[0].shape
    count = len(parts)

    def body(given, outs):
        for k in range(count):
            outs[0][pl.ds(pl.multiple_of(given[0][k] * share, share), share), :] = given[1 + k][...]

    return small_kernel(body, "place_parts", [order], parts, f32(share * count, width), after)


def copy_rows(value, pieces, after):
    def body(given, outs):
        for (first, count), out in zip(pieces, outs):
            out[...] = given[0][first : first + count, :]

    shapes = [jax.ShapeDtypeStruct((count, value.shape[1]), value.dtype) for _, count in pieces]
    return small_kernel(body, "copy_rows", [], [value], shapes, after)


def live_halves(which, cell_counts, embeddings):
    slots, width = embeddings.shape
    half = slots // 2

    def body(given, outs):
        which_ref, count_ref, x_ref = given
        for out, part in zip(outs, (which_ref[0], 1 - which_ref[0])):
            first = pl.multiple_of(part * half, half)
            row = first + lax.broadcasted_iota(jnp.int32, (half, width), 0)
            values = x_ref[pl.ds(first, half), :]
            out[...] = jnp.where(row < count_ref[0], values.astype(jnp.float32), 0.0).astype(values.dtype)

    shape = jax.ShapeDtypeStruct((half, width), embeddings.dtype)
    return small_kernel(body, "live_halves", [which, cell_counts], [embeddings], [shape] * 2)


def join_features(which, mine, other):
    rows, width = mine.shape

    def body(given, outs):
        which_ref, mine_ref, other_ref = given
        first = which_ref[0] == 0
        values = mine_ref[...], other_ref[...]
        outs[0][:, :width] = jnp.where(first, values[0], values[1])
        outs[0][:, width:] = jnp.where(first, values[1], values[0])

    return small_kernel(
        body, "join_features", [which], [mine, other], jax.ShapeDtypeStruct((rows, 2 * width), mine.dtype)
    )


def choose(which, zero, one, after=()):
    def body(given, outs):
        outs[0][...] = jnp.where(given[0][0] == 1, given[2][...], given[1][...])

    return small_kernel(
        body, "choose", [which], [zero, one], jax.ShapeDtypeStruct(zero.shape, zero.dtype), after
    )


def factor_step(step, value, after=()):
    width = value.shape[0]
    body = lambda given, outs: factor_kernel(step, width // TILE, given[0], outs[0])
    return small_kernel(body, "factor_step", [], [value], f32(width, width), after, moved=FACTOR_BYTES)


def gram_inverse(value, scale, after=()):
    width = value.shape[0]

    def body(given, outs):
        down = lax.broadcasted_iota(jnp.int32, (width, width), 0)
        across = lax.broadcasted_iota(jnp.int32, (width, width), 1)
        lower = jnp.where(down >= across, given[0][...], 0.0)
        outs[0][...] = scale * lax.dot_general(
            lower, lower, (((0,), (0,)), ((), ())), precision=HI, preferred_element_type=jnp.float32
        )

    return small_kernel(body, "gram_inverse", [], [value], f32(width, width), after)


def apply_inverse(inverse, parts):
    width = inverse.shape[0]
    rows = parts[0].shape[0]

    def body(given, outs):
        cross = (given[1][...] + given[2][...]) + (given[3][...] + given[4][...])
        outs[0][...] = lax.dot_general(
            given[0][...], cross, (((1,), (1,)), ((), ())), precision=HI, preferred_element_type=jnp.float32
        )

    return small_kernel(body, "apply_inverse", [], [inverse, *parts], f32(width, rows))


def shards(embeddings, targets_by_gene, cell_counts):
    slots = embeddings.shape[0]
    donors = lax.axis_size("donor")
    donor = lax.axis_index("donor")
    c = lax.axis_index("gene")
    z, y, x = donor // 4, (donor // 2) % 2, donor % 2
    near_bit = jnp.where(c == 0, x, y)
    far_bit = jnp.where(c == 0, y, x)
    half = slots // 2
    ints = lambda *values: jnp.stack(values).astype(jnp.int32)

    def group_donor(k, core, bit):
        line, other = k // 2, k % 2
        return line * 4 + jnp.where(core == 0, other * 2 + bit, bit * 2 + other)

    ks = jnp.arange(8, dtype=jnp.int32)

    def blocks_for(core, bit):
        return (group_donor(ks, core, bit) * 2 + core).astype(jnp.int32)

    core = ints(c)
    keep, give = live_halves(core, cell_counts, embeddings)
    got = send(give, CORE)
    block = join_features(core, keep, got)
    rows = targets_by_gene.shape[0]
    line1 = send(block, LINE[0])
    far_own = send(block, FAR)

    gram_give = gram_rows(ints(1 - c), block)
    gram_got = send(gram_give, CORE)
    gram_keep = gram_rows(ints(c), block, after=(gram_give,))
    place = donor % 4
    order = ints(place, place ^ 1, place ^ 2, place ^ 3)
    mine, *others = add_split(order, [gram_keep, gram_got])
    parts = [mine] + [send(other, PLANE[s]) for s, other in enumerate(others)]
    plane_sum = add_all(parts, after=(far_own,))
    near_low = pick_blocks(targets_by_gene, blocks_for(c, 1 - near_bit), half, (plane_sum,), 0, rows // 2)
    near_low = send(near_low, NEAR)

    line_parts = [plane_sum] + [send(plane_sum, LINE[s]) for s in range(3)]
    total = add_all(line_parts, after=(line1,))

    quarters = [total] + [send(total, PLANE[s]) for s in range(3)]
    (late,) = copy_rows(block, ((0, half),), (total,))
    middle_own = send(late, MIDDLE)
    quarter = place_parts(order, quarters, (late,))
    (late,) = copy_rows(line1, ((0, half),), (quarter,))
    middle_outer = send(late, MIDDLE)
    near_high = pick_blocks(
        targets_by_gene, blocks_for(c, 1 - near_bit), half, (late,), rows // 2, rows // 2
    )
    gram = place_parts(ints(c, 1 - c), [quarter, send(quarter, CORE)], after=(near_high, near_low))
    near_high = send(near_high, NEAR)
    value = factor_step(0, gram)
    for_diag = pick_blocks(targets_by_gene, blocks_for(1 - c, 1 - far_bit), half, (value,))
    from_diag = send(for_diag, DIAG_OUT)
    for_core = pick_blocks(targets_by_gene, blocks_for(1 - c, far_bit), half, after=(for_diag,))
    from_core = send(for_core, CORE)

    value = factor_step(1, value, after=(for_core,))
    (late,) = copy_rows(middle_own, ((0, half),), (value, near_high))
    outward_own = send(late, OUTWARD)
    (late,) = copy_rows(line1, ((0, half),), (late,))
    far1 = send(late, FAR)
    value = factor_step(2, value, after=(late,))
    value = factor_step(3, value)
    inverse = gram_inverse(value, math.sqrt(slots * donors))
    (late,) = copy_rows(middle_outer, ((0, half),), (inverse,))
    outward_outer = send(late, OUTWARD)
    is_middle = jnp.where((z == 1) | (z == 2), 1, 0)
    second = choose(ints(is_middle), outward_own, middle_own, (late,))
    far2 = send(second, FAR)
    third = choose(ints(is_middle), outward_outer, middle_outer)
    far3 = send(third, FAR)
    second_z = jnp.where(is_middle == 1, z ^ 3, z ^ 2)
    third_z = jnp.where(is_middle == 1, z ^ 2, z ^ 3)

    def cells_of(piece, cells_z, other, part=0):
        k = cells_z * 2 + other
        column = (group_donor(k, c, near_bit) * 2 + c) * (half // piece.shape[0]) + part
        return piece, column, k, part

    received = (from_core, near_low, near_high, from_diag)
    acc = None
    for blocks in (
        [(block, z, far_bit), (far_own, z, 1 - far_bit), (line1, z ^ 1, far_bit)],
        [(second, second_z, far_bit), (far1, z ^ 1, 1 - far_bit)],
        [(third, third_z, far_bit), (far2, second_z, 1 - far_bit)],
        [(far3, third_z, 1 - far_bit)],
    ):
        acc = cross_add(
            acc, targets_by_gene, received, [cells_of(*block) for block in blocks], (inverse,) if acc is None else ()
        )
    own, for_other, to_near, to_diag = acc
    scaled = apply_inverse(
        inverse, [own, send(for_other, CORE), send(to_near, NEAR), send(to_diag, DIAG_BACK)]
    )
    return lax.all_to_all(scaled, "donor", split_axis=0, concat_axis=1, tiled=True)


def solution(mesh):
    placed = (P("donor", "gene"), P(("gene", "donor"), None), P("donor"))
    tuned = mesh.shape["donor"] == 16 and mesh.shape["gene"] == 2
    return jax.shard_map(
        shards if tuned else shards_any_mesh,
        mesh=mesh,
        in_specs=placed,
        out_specs=P("donor", "gene"),
        check_vma=False,
    )
```

```python
import functools
import math

import jax
import jax.numpy as jnp
from jax import lax
from jax.experimental import pallas as pl
from jax.experimental.pallas import tpu as pltpu
from jax.sharding import PartitionSpec as P

AXES = ("donor", "gene")
HI = lax.Precision.HIGHEST
VMEM_BYTES = 48 * 1024 * 1024
FACTOR_BYTES = 1


def solve_both(lower_factor, right_cols):
    halfway = lax.linalg.triangular_solve(lower_factor, right_cols, left_side=True, lower=True)
    return lax.linalg.triangular_solve(
        lower_factor, halfway, left_side=True, lower=True, transpose_a=True
    )


def shards_any_mesh(embeddings, targets_by_gene, cell_counts):
    valid_count = cell_counts[0]
    gathered = lax.all_gather(embeddings, "gene", axis=1, tiled=True)
    row_total = gathered.shape[0]
    width = gathered.shape[1]
    donors = lax.axis_size("donor")
    row_valid = lax.broadcasted_iota(jnp.int32, (row_total, 1), 0) < valid_count
    masked = jnp.where(row_valid, gathered, jnp.zeros_like(gathered))
    gram_matrix = lax.dot_general(
        masked, masked, (((0,), (0,)), ((), ())), preferred_element_type=jnp.float32
    )
    by_rows = lax.all_to_all(targets_by_gene, "donor", split_axis=1, concat_axis=0, tiled=True)
    gram_matrix = lax.psum(gram_matrix, "donor")
    lower_factor = jnp.linalg.cholesky(gram_matrix)
    scale_total = math.sqrt(row_total * donors)
    cross_local = jnp.dot(by_rows, masked, preferred_element_type=jnp.float32)
    cross_sum = lax.psum(cross_local, "donor")
    scaled = scale_total * solve_both(lower_factor, cross_sum.T)
    share = width // donors
    first_row = lax.axis_index("donor") * share
    return lax.dynamic_slice_in_dim(scaled, first_row, share, 0)


def permutation(target):
    pairs = []
    for z in range(4):
        for y in range(2):
            for x in range(2):
                for c in range(2):
                    there = target(z, y, x, c)
                    if there is not None:
                        tz, ty, tx, tc = there
                        pairs.append((((z * 2 + y) * 2 + x) * 2 + c, ((tz * 2 + ty) * 2 + tx) * 2 + tc))
    return pairs


CORE = permutation(lambda z, y, x, c: (z, y, x, 1 - c))
NEAR = permutation(lambda z, y, x, c: (z, y, 1 - x, c) if c == 0 else (z, 1 - y, x, c))
FAR = permutation(lambda z, y, x, c: (z, 1 - y, x, c) if c == 0 else (z, y, 1 - x, c))
DIAG_OUT = permutation(lambda z, y, x, c: (z, 1 - y, x, 1) if c == 0 else (z, y, 1 - x, 0))
DIAG_BACK = permutation(lambda z, y, x, c: (z, y, 1 - x, 1) if c == 0 else (z, 1 - y, x, 0))
PLANE = [permutation(lambda z, y, x, c, s=s: (z, y ^ (s >> 1), x ^ (s & 1), c)) for s in (1, 2, 3)]
LINE = [permutation(lambda z, y, x, c, s=s: (z ^ s, y, x, c)) for s in (1, 2, 3)]

MIDDLE = permutation(lambda z, y, x, c: (3 - z, y, x, c) if z in (1, 2) else None)
OUTWARD = permutation(lambda z, y, x, c: (z ^ 1, y, x, c) if z in (1, 2) else None)


def send(value, perm):
    return lax.ppermute(value, AXES, perm)


def pick_kernel(first_row, index_ref, t_ref, *rest):
    o_ref, held, in_sems, out_sems = rest[-4:]
    count, rows, block_cells = held.shape
    copies = []
    for k in range(count):
        start = pl.multiple_of(index_ref[k] * block_cells, block_cells)
        copies.append(
            (
                pltpu.make_async_copy(t_ref.at[first_row : first_row + rows, pl.ds(start, block_cells)], held.at[k], in_sems.at[k]),
                pltpu.make_async_copy(held.at[k], o_ref.at[k], out_sems.at[k]),
            )
        )
    for inward, _ in copies:
        inward.start()
    for inward, outward in copies:
        inward.wait()
        outward.start()
    for _, outward in copies:
        outward.wait()


def pick_blocks(targets, block_index, block_cells, after=(), first_row=0, rows=None):
    rows = rows or targets.shape[0]
    count = block_index.shape[0]
    return pl.pallas_call(
        functools.partial(pick_kernel, first_row),
        out_shape=jax.ShapeDtypeStruct((count, rows, block_cells), targets.dtype),
        in_specs=[pl.BlockSpec(memory_space=pltpu.SMEM)]
        + [pl.BlockSpec(memory_space=pl.ANY)] * (1 + len(after)),
        out_specs=pl.BlockSpec(memory_space=pl.ANY),
        scratch_shapes=[
            pltpu.VMEM((count, rows, block_cells), targets.dtype),
            pltpu.SemaphoreType.DMA((count,)),
            pltpu.SemaphoreType.DMA((count,)),
        ],
        compiler_params=pltpu.CompilerParams(vmem_limit_bytes=VMEM_BYTES),
        cost_estimate=pl.CostEstimate(flops=1, bytes_accessed=1, transcendentals=0),
        name="pick_blocks",
    )(block_index, targets, *after)


def cross_kernel(has_prior, blocks, index_ref, *refs):
    outs = refs[-4:]
    prior = refs[6 * blocks : 6 * blocks + 4]
    rows = outs[0].shape[0]
    total = None
    for n in range(blocks):
        own, from_core, near_low, near_high, from_diag, x_ref = refs[6 * n : 6 * n + 6]
        pieces = [own[...], from_core[0], near_low[0], near_high[0], from_diag[0]]
        part = jnp.dot(jnp.concatenate(pieces, axis=0), x_ref[...], preferred_element_type=jnp.float32)
        total = part if total is None else total + part
    for q in range(4):
        part = total[q * rows : (q + 1) * rows, :]
        outs[q][...] = part + prior[q][...] if has_prior else part


def cross_add(prior, targets, received, blocks, after=()):
    rows = targets.shape[0]
    whole = lambda shape: pl.BlockSpec(shape, lambda i, index: (0, 0))
    index, operands, in_specs = [], [], []
    for n, (block, column, slot, part) in enumerate(blocks):
        cells, width = block.shape
        index += [column, slot]
        operands += [targets, *received, block]
        in_specs += [pl.BlockSpec((rows, cells), lambda i, index, n=n: (0, index[2 * n]))]
        in_specs += [
            pl.BlockSpec((1, value.shape[1], cells), lambda i, index, n=n, part=part: (index[2 * n + 1], 0, part))
            for value in received
        ]
        in_specs += [whole((cells, width))]
    sums = [whole((rows, width))] * 4
    aliases = {1 + len(operands) + q: q for q in range(4)} if prior else {}
    return pl.pallas_call(
        functools.partial(cross_kernel, prior is not None, len(blocks)),
        out_shape=[jax.ShapeDtypeStruct((rows, width), jnp.float32)] * 4,
        grid_spec=pltpu.PrefetchScalarGridSpec(
            num_scalar_prefetch=1,
            grid=(1,),
            in_specs=in_specs + (sums if prior else []) + [pl.BlockSpec(memory_space=pl.ANY)] * len(after),
            out_specs=sums,
        ),
        input_output_aliases=aliases,
        compiler_params=pltpu.CompilerParams(vmem_limit_bytes=VMEM_BYTES),
        cost_estimate=pl.CostEstimate(flops=1, bytes_accessed=1, transcendentals=0),
        name="cross_add",
    )(jnp.stack(index).astype(jnp.int32), *operands, *(prior or ()), *after)


TILE = 128
SUB = 8


def inverse_root(value):
    root = lax.rsqrt(value)
    return root * (1.5 - 0.5 * value * root * root)


def factor_tiles(tiles):
    lane = lax.broadcasted_iota(jnp.int32, (SUB, TILE), 1)
    sub = lax.broadcasted_iota(jnp.int32, (SUB, TILE), 0)
    wide = lambda value: jnp.broadcast_to(value, (SUB, TILE))
    count = len(tiles)
    for p in range(count):
        low = p * SUB
        inside = (lane >= low) & (lane < low + SUB)
        rows = tiles[p]
        cols = [wide(rows[:, low + k : low + k + 1]) for k in range(SUB)]
        below = [[wide(tiles[i][:, low + k : low + k + 1]) for k in range(SUB)] for i in range(p + 1, count)]
        rows = jnp.where(inside, jnp.where(lane - low == sub, 1.0, 0.0), rows)
        for i in range(p + 1, count):
            tiles[i] = jnp.where(inside, 0.0, tiles[i])
        for k in range(SUB):
            root = inverse_root(wide(cols[k][k : k + 1, :]))
            scaled = cols[k] * root
            factors = {j: wide(scaled[j : j + 1, :]) for j in range(k + 1, SUB)}
            for j in range(k + 1, SUB):
                cols[j] = cols[j] - scaled * factors[j]
            pivot_row = wide(rows[k : k + 1, :]) * root
            rows = jnp.where(sub == k, pivot_row, jnp.where(sub > k, rows - scaled * pivot_row, rows))
            for i in range(p + 1, count):
                mine = below[i - p - 1]
                scaled_below = mine[k] * root
                for j in range(k + 1, SUB):
                    mine[j] = mine[j] - scaled_below * factors[j]
                tiles[i] = tiles[i] - scaled_below * pivot_row
        tiles[p] = rows
    return jnp.concatenate(tiles, axis=0)


def factor_kernel(step, count, v_ref, o_ref):
    here = slice(step * TILE, (step + 1) * TILE)
    o_ref[...] = v_ref[...]
    inverse = factor_tiles([v_ref[step * TILE + i * SUB : step * TILE + (i + 1) * SUB, here] for i in range(TILE // SUB)])
    down = lax.broadcasted_iota(jnp.int32, (TILE, TILE), 0)
    across = lax.broadcasted_iota(jnp.int32, (TILE, TILE), 1)
    inverse = jnp.where(down >= across, inverse, 0.0)
    o_ref[here, :] = jnp.dot(inverse, v_ref[here, :], precision=HI, preferred_element_type=jnp.float32)
    o_ref[here, here] = inverse
    if step + 1 < count:
        below = slice((step + 1) * TILE, count * TILE)
        o_ref[below, here] = jnp.zeros((TILE * (count - step - 1), TILE), jnp.float32)
        o_ref[below, :] = o_ref[below, :] - lax.dot_general(
            o_ref[here, below], o_ref[here, :], (((0,), (0,)), ((), ())), precision=HI, preferred_element_type=jnp.float32
        )


ANYWHERE = pl.BlockSpec(memory_space=pl.ANY)
SCALARS = pl.BlockSpec(memory_space=pltpu.SMEM)
VECTORS = pl.BlockSpec(memory_space=pltpu.VMEM)


def small_kernel(body, name, scalars, values, out_shape, after=(), moved=1):
    def kernel(*refs):
        given = len(scalars) + len(values)
        body(refs[:given], refs[given + len(after) :])

    return pl.pallas_call(
        kernel,
        out_shape=out_shape,
        in_specs=[SCALARS] * len(scalars) + [VECTORS] * len(values) + [ANYWHERE] * len(after),
        compiler_params=pltpu.CompilerParams(vmem_limit_bytes=VMEM_BYTES),
        cost_estimate=pl.CostEstimate(flops=1, bytes_accessed=moved, transcendentals=0),
        name=name,
    )(*scalars, *values, *after)


def f32(*shape):
    return jax.ShapeDtypeStruct(shape, jnp.float32)


def gram_rows(which, block, after=()):
    cells, width = block.shape
    half = width // 2

    def body(given, outs):
        which_ref, x_ref = given
        columns = x_ref[:, pl.ds(pl.multiple_of(which_ref[0] * half, half), half)]
        outs[0][...] = lax.dot_general(
            columns, x_ref[...], (((0,), (0,)), ((), ())), preferred_element_type=jnp.float32
        )

    return small_kernel(body, "gram_rows", [which], [block], f32(half, width), after)


def add_split(order, parts, after=()):
    rows, width = parts[0].shape
    count = order.shape[0]
    share = rows // count

    def body(given, outs):
        order_ref, part_refs = given[0], given[1:]
        for k in range(count):
            place = pl.ds(pl.multiple_of(order_ref[k] * share, share), share)
            total = part_refs[0][place, :]
            for ref in part_refs[1:]:
                total = total + ref[place, :]
            outs[k][...] = total

    return small_kernel(body, "add_split", [order], parts, [f32(share, width)] * count, after)


def add_all(parts, after=()):
    def body(given, outs):
        total = given[0][...]
        for ref in given[1:]:
            total = total + ref[...]
        outs[0][...] = total

    return small_kernel(body, "add_all", [], parts, f32(*parts[0].shape), after)


def place_parts(order, parts, after=()):
    share, width = parts[0].shape
    count = len(parts)

    def body(given, outs):
        for k in range(count):
            outs[0][pl.ds(pl.multiple_of(given[0][k] * share, share), share), :] = given[1 + k][...]

    return small_kernel(body, "place_parts", [order], parts, f32(share * count, width), after)


def copy_rows(value, pieces, after):
    def body(given, outs):
        for (first, count), out in zip(pieces, outs):
            out[...] = given[0][first : first + count, :]

    shapes = [jax.ShapeDtypeStruct((count, value.shape[1]), value.dtype) for _, count in pieces]
    return small_kernel(body, "copy_rows", [], [value], shapes, after)


def live_halves(which, cell_counts, embeddings):
    slots, width = embeddings.shape
    half = slots // 2

    def body(given, outs):
        which_ref, count_ref, x_ref = given
        for out, part in zip(outs, (which_ref[0], 1 - which_ref[0])):
            first = pl.multiple_of(part * half, half)
            row = first + lax.broadcasted_iota(jnp.int32, (half, width), 0)
            values = x_ref[pl.ds(first, half), :]
            out[...] = jnp.where(row < count_ref[0], values.astype(jnp.float32), 0.0).astype(values.dtype)

    shape = jax.ShapeDtypeStruct((half, width), embeddings.dtype)
    return small_kernel(body, "live_halves", [which, cell_counts], [embeddings], [shape] * 2)


def join_features(which, mine, other):
    rows, width = mine.shape

    def body(given, outs):
        which_ref, mine_ref, other_ref = given
        first = which_ref[0] == 0
        values = mine_ref[...], other_ref[...]
        outs[0][:, :width] = jnp.where(first, values[0], values[1])
        outs[0][:, width:] = jnp.where(first, values[1], values[0])

    return small_kernel(
        body, "join_features", [which], [mine, other], jax.ShapeDtypeStruct((rows, 2 * width), mine.dtype)
    )


def choose(which, zero, one, after=()):
    def body(given, outs):
        outs[0][...] = jnp.where(given[0][0] == 1, given[2][...], given[1][...])

    return small_kernel(
        body, "choose", [which], [zero, one], jax.ShapeDtypeStruct(zero.shape, zero.dtype), after
    )


def factor_step(step, value, after=()):
    width = value.shape[0]
    body = lambda given, outs: factor_kernel(step, width // TILE, given[0], outs[0])
    return small_kernel(body, "factor_step", [], [value], f32(width, width), after, moved=FACTOR_BYTES)


def gram_inverse(value, scale, after=()):
    width = value.shape[0]

    def body(given, outs):
        down = lax.broadcasted_iota(jnp.int32, (width, width), 0)
        across = lax.broadcasted_iota(jnp.int32, (width, width), 1)
        lower = jnp.where(down >= across, given[0][...], 0.0)
        outs[0][...] = scale * lax.dot_general(
            lower, lower, (((0,), (0,)), ((), ())), precision=HI, preferred_element_type=jnp.float32
        )

    return small_kernel(body, "gram_inverse", [], [value], f32(width, width), after)


def apply_inverse(inverse, parts):
    width = inverse.shape[0]
    rows = parts[0].shape[0]

    def body(given, outs):
        cross = (given[1][...] + given[2][...]) + (given[3][...] + given[4][...])
        outs[0][...] = lax.dot_general(
            given[0][...], cross, (((1,), (1,)), ((), ())), precision=HI, preferred_element_type=jnp.float32
        )

    return small_kernel(body, "apply_inverse", [], [inverse, *parts], f32(width, rows))


def shards(embeddings, targets_by_gene, cell_counts):
    slots = embeddings.shape[0]
    donors = lax.axis_size("donor")
    donor = lax.axis_index("donor")
    c = lax.axis_index("gene")
    z, y, x = donor // 4, (donor // 2) % 2, donor % 2
    near_bit = jnp.where(c == 0, x, y)
    far_bit = jnp.where(c == 0, y, x)
    half = slots // 2
    ints = lambda *values: jnp.stack(values).astype(jnp.int32)

    def group_donor(k, core, bit):
        line, other = k // 2, k % 2
        return line * 4 + jnp.where(core == 0, other * 2 + bit, bit * 2 + other)

    ks = jnp.arange(8, dtype=jnp.int32)

    def blocks_for(core, bit):
        return (group_donor(ks, core, bit) * 2 + core).astype(jnp.int32)

    core = ints(c)
    keep, give = live_halves(core, cell_counts, embeddings)
    got = send(give, CORE)
    block = join_features(core, keep, got)
    line1 = send(block, LINE[0])
    middle_own = send(block, MIDDLE)
    far_own = send(block, FAR)

    gram_give = gram_rows(ints(1 - c), block)
    gram_got = send(gram_give, CORE)
    gram_keep = gram_rows(ints(c), block, after=(gram_give,))
    mine, give = add_split(ints(near_bit, 1 - near_bit), [gram_keep, gram_got])
    for_core = pick_blocks(targets_by_gene, blocks_for(1 - c, far_bit), half, after=(mine,))
    from_core = send(for_core, CORE)
    mine, give = add_split(ints(far_bit, 1 - far_bit), [mine, send(give, NEAR)], after=(for_core,))
    got = send(give, FAR)
    place = near_bit * 2 + far_bit
    order = ints(place, place ^ jnp.where(c == 0, 2, 1), place ^ jnp.where(c == 0, 1, 2), place ^ 3)

    rows = targets_by_gene.shape[0]
    cut = 6 * rows // 10 // 16 * 16
    near_blocks = blocks_for(c, 1 - near_bit)
    for_near = pick_blocks(targets_by_gene, near_blocks, half, (got, far_own, line1, middle_own), 0, cut)
    near_low = send(for_near, NEAR)
    plane_sum = add_all([mine, got], after=(line1, middle_own))
    line_parts = [plane_sum] + [send(plane_sum, LINE[s]) for s in range(3)]
    total = add_all(line_parts)

    quarters = [total] + [send(total, PLANE[s]) for s in range(3)]
    for_near = pick_blocks(targets_by_gene, near_blocks, half, (total,), cut, rows - cut)
    near_high = send(for_near, NEAR)
    quarter = place_parts(order, quarters, (for_near, near_low, from_core))
    outward_own = send(middle_own, OUTWARD)
    middle_outer = send(line1, MIDDLE)
    for_diag = pick_blocks(targets_by_gene, blocks_for(1 - c, 1 - far_bit), half, (quarter,))
    from_diag = send(for_diag, DIAG_OUT)
    gram = place_parts(ints(c, 1 - c), [quarter, send(quarter, CORE)], after=(for_diag,))

    value = factor_step(0, gram)
    value = factor_step(1, value)
    (late,) = copy_rows(middle_outer, ((0, half),), (value, near_high, outward_own))
    outward_outer = send(late, OUTWARD)
    (late,) = copy_rows(line1, ((0, half),), (late,))
    far1 = send(late, FAR)
    is_middle = jnp.where((z == 1) | (z == 2), 1, 0)
    second = choose(ints(is_middle), outward_own, middle_own, (late,))
    far2 = send(second, FAR)
    value = factor_step(2, value, after=(second,))
    value = factor_step(3, value)
    inverse = gram_inverse(value, math.sqrt(slots * donors))
    second_z = jnp.where(is_middle == 1, z ^ 3, z ^ 2)
    third_z = jnp.where(is_middle == 1, z ^ 2, z ^ 3)

    def cells_of(piece, cells_z, other, part=0):
        k = cells_z * 2 + other
        column = (group_donor(k, c, near_bit) * 2 + c) * (half // piece.shape[0]) + part
        return piece, column, k, part

    received = (from_core, near_low, near_high, from_diag)
    def add(acc, blocks, after=()):
        return cross_add(acc, targets_by_gene, received, [cells_of(*block) for block in blocks], after)

    acc = add(None, [(block, z, far_bit), (far_own, z, 1 - far_bit), (line1, z ^ 1, far_bit)], (inverse,))
    acc = add(acc, [(second, second_z, far_bit), (far1, z ^ 1, 1 - far_bit)])
    third = choose(ints(is_middle), outward_outer, middle_outer, (inverse,))
    far3 = send(third, FAR)
    acc = add(acc, [(third, third_z, far_bit), (far2, second_z, 1 - far_bit)])
    acc = add(acc, [(far3, third_z, 1 - far_bit)])
    own, for_other, to_near, to_diag = acc
    scaled = apply_inverse(
        inverse, [own, send(for_other, CORE), send(to_near, NEAR), send(to_diag, DIAG_BACK)]
    )
    return lax.all_to_all(scaled, "donor", split_axis=0, concat_axis=1, tiled=True)


def solution(mesh):
    placed = (P("donor", "gene"), P(("gene", "donor"), None), P("donor"))
    tuned = mesh.shape["donor"] == 16 and mesh.shape["gene"] == 2
    return jax.shard_map(
        shards if tuned else shards_any_mesh,
        mesh=mesh,
        in_specs=placed,
        out_specs=P("donor", "gene"),
        check_vma=False,
    )
```

```python
import functools
import math

import jax
import jax.numpy as jnp
from jax import lax
from jax.experimental import pallas as pl
from jax.experimental.pallas import tpu as pltpu
from jax.sharding import PartitionSpec as P

AXES = ("donor", "gene")
HI = lax.Precision.HIGHEST
VMEM_BYTES = 40 * 1024 * 1024
FACTOR_BYTES = 1


def solve_both(lower_factor, right_cols):
    halfway = lax.linalg.triangular_solve(lower_factor, right_cols, left_side=True, lower=True)
    return lax.linalg.triangular_solve(
        lower_factor, halfway, left_side=True, lower=True, transpose_a=True
    )


def shards_any_mesh(embeddings, targets_by_gene, cell_counts):
    valid_count = cell_counts[0]
    gathered = lax.all_gather(embeddings, "gene", axis=1, tiled=True)
    row_total = gathered.shape[0]
    width = gathered.shape[1]
    donors = lax.axis_size("donor")
    row_valid = lax.broadcasted_iota(jnp.int32, (row_total, 1), 0) < valid_count
    masked = jnp.where(row_valid, gathered, jnp.zeros_like(gathered))
    gram_matrix = lax.dot_general(
        masked, masked, (((0,), (0,)), ((), ())), preferred_element_type=jnp.float32
    )
    by_rows = lax.all_to_all(targets_by_gene, "donor", split_axis=1, concat_axis=0, tiled=True)
    gram_matrix = lax.psum(gram_matrix, "donor")
    lower_factor = jnp.linalg.cholesky(gram_matrix)
    scale_total = math.sqrt(row_total * donors)
    cross_local = jnp.dot(by_rows, masked, preferred_element_type=jnp.float32)
    cross_sum = lax.psum(cross_local, "donor")
    scaled = scale_total * solve_both(lower_factor, cross_sum.T)
    share = width // donors
    first_row = lax.axis_index("donor") * share
    return lax.dynamic_slice_in_dim(scaled, first_row, share, 0)


def permutation(target):
    pairs = []
    for z in range(4):
        for y in range(2):
            for x in range(2):
                for c in range(2):
                    there = target(z, y, x, c)
                    if there is not None:
                        tz, ty, tx, tc = there
                        pairs.append((((z * 2 + y) * 2 + x) * 2 + c, ((tz * 2 + ty) * 2 + tx) * 2 + tc))
    return pairs


CORE = permutation(lambda z, y, x, c: (z, y, x, 1 - c))
NEAR = permutation(lambda z, y, x, c: (z, y, 1 - x, c) if c == 0 else (z, 1 - y, x, c))
FAR = permutation(lambda z, y, x, c: (z, 1 - y, x, c) if c == 0 else (z, y, 1 - x, c))
DIAG_OUT = permutation(lambda z, y, x, c: (z, 1 - y, x, 1) if c == 0 else (z, y, 1 - x, 0))
DIAG_BACK = permutation(lambda z, y, x, c: (z, y, 1 - x, 1) if c == 0 else (z, 1 - y, x, 0))
PLANE = [permutation(lambda z, y, x, c, s=s: (z, y ^ (s >> 1), x ^ (s & 1), c)) for s in (1, 2, 3)]
LINE = [permutation(lambda z, y, x, c, s=s: (z ^ s, y, x, c)) for s in (1, 2, 3)]

MIDDLE = permutation(lambda z, y, x, c: (3 - z, y, x, c) if z in (1, 2) else None)
OUTWARD = permutation(lambda z, y, x, c: (z ^ 1, y, x, c) if z in (1, 2) else None)


def send(value, perm):
    return lax.ppermute(value, AXES, perm)


def pick_kernel(first_row, index_ref, t_ref, *rest):
    o_ref, held, in_sems, out_sems = rest[-4:]
    count, rows, block_cells = held.shape
    copies = []
    for k in range(count):
        start = pl.multiple_of(index_ref[k] * block_cells, block_cells)
        copies.append(
            (
                pltpu.make_async_copy(t_ref.at[first_row : first_row + rows, pl.ds(start, block_cells)], held.at[k], in_sems.at[k]),
                pltpu.make_async_copy(held.at[k], o_ref.at[k], out_sems.at[k]),
            )
        )
    for inward, _ in copies:
        inward.start()
    for inward, outward in copies:
        inward.wait()
        outward.start()
    for _, outward in copies:
        outward.wait()


def pick_blocks(targets, block_index, block_cells, after=(), first_row=0, rows=None):
    rows = rows or targets.shape[0]
    count = block_index.shape[0]
    return pl.pallas_call(
        functools.partial(pick_kernel, first_row),
        out_shape=jax.ShapeDtypeStruct((count, rows, block_cells), targets.dtype),
        in_specs=[pl.BlockSpec(memory_space=pltpu.SMEM)]
        + [pl.BlockSpec(memory_space=pl.ANY)] * (1 + len(after)),
        out_specs=pl.BlockSpec(memory_space=pl.ANY),
        scratch_shapes=[
            pltpu.VMEM((count, rows, block_cells), targets.dtype),
            pltpu.SemaphoreType.DMA((count,)),
            pltpu.SemaphoreType.DMA((count,)),
        ],
        compiler_params=pltpu.CompilerParams(vmem_limit_bytes=VMEM_BYTES),
        cost_estimate=pl.CostEstimate(flops=1, bytes_accessed=1, transcendentals=0),
        name="pick_blocks",
    )(block_index, targets, *after)


def cross_kernel(has_prior, blocks, index_ref, *refs):
    outs = refs[-4:]
    prior = refs[6 * blocks : 6 * blocks + 4]
    rows = outs[0].shape[0]
    total = None
    for n in range(blocks):
        own, from_core, near_low, near_high, from_diag, x_ref = refs[6 * n : 6 * n + 6]
        pieces = [own[...], from_core[0], near_low[0], near_high[0], from_diag[0]]
        part = jnp.dot(jnp.concatenate(pieces, axis=0), x_ref[...], preferred_element_type=jnp.float32)
        total = part if total is None else total + part
    for q in range(4):
        part = total[q * rows : (q + 1) * rows, :]
        outs[q][...] = part + prior[q][...] if has_prior else part


def cross_add(prior, targets, received, blocks, after=()):
    rows = targets.shape[0]
    whole = lambda shape: pl.BlockSpec(shape, lambda i, index: (0, 0))
    index, operands, in_specs = [], [], []
    for n, (block, column, slot, part) in enumerate(blocks):
        cells, width = block.shape
        index += [column, slot]
        operands += [targets, *received, block]
        in_specs += [pl.BlockSpec((rows, cells), lambda i, index, n=n: (0, index[2 * n]))]
        in_specs += [
            pl.BlockSpec((1, value.shape[1], cells), lambda i, index, n=n, part=part: (index[2 * n + 1], 0, part))
            for value in received
        ]
        in_specs += [whole((cells, width))]
    sums = [whole((rows, width))] * 4
    aliases = {1 + len(operands) + q: q for q in range(4)} if prior else {}
    return pl.pallas_call(
        functools.partial(cross_kernel, prior is not None, len(blocks)),
        out_shape=[jax.ShapeDtypeStruct((rows, width), jnp.float32)] * 4,
        grid_spec=pltpu.PrefetchScalarGridSpec(
            num_scalar_prefetch=1,
            grid=(1,),
            in_specs=in_specs + (sums if prior else []) + [pl.BlockSpec(memory_space=pl.ANY)] * len(after),
            out_specs=sums,
        ),
        input_output_aliases=aliases,
        compiler_params=pltpu.CompilerParams(vmem_limit_bytes=VMEM_BYTES),
        cost_estimate=pl.CostEstimate(flops=1, bytes_accessed=1, transcendentals=0),
        name="cross_add",
    )(jnp.stack(index).astype(jnp.int32), *operands, *(prior or ()), *after)


TILE = 128
SUB = 8


def inverse_root(value):
    root = lax.rsqrt(value)
    return root * (1.5 - 0.5 * value * root * root)


def factor_tiles(tiles):
    lane = lax.broadcasted_iota(jnp.int32, (SUB, TILE), 1)
    sub = lax.broadcasted_iota(jnp.int32, (SUB, TILE), 0)
    wide = lambda value: jnp.broadcast_to(value, (SUB, TILE))
    count = len(tiles)
    for p in range(count):
        low = p * SUB
        inside = (lane >= low) & (lane < low + SUB)
        rows = tiles[p]
        cols = [wide(rows[:, low + k : low + k + 1]) for k in range(SUB)]
        below = [[wide(tiles[i][:, low + k : low + k + 1]) for k in range(SUB)] for i in range(p + 1, count)]
        rows = jnp.where(inside, jnp.where(lane - low == sub, 1.0, 0.0), rows)
        for i in range(p + 1, count):
            tiles[i] = jnp.where(inside, 0.0, tiles[i])
        for k in range(SUB):
            root = inverse_root(wide(cols[k][k : k + 1, :]))
            scaled = cols[k] * root
            factors = {j: wide(scaled[j : j + 1, :]) for j in range(k + 1, SUB)}
            for j in range(k + 1, SUB):
                cols[j] = cols[j] - scaled * factors[j]
            pivot_row = wide(rows[k : k + 1, :]) * root
            rows = jnp.where(sub == k, pivot_row, jnp.where(sub > k, rows - scaled * pivot_row, rows))
            for i in range(p + 1, count):
                mine = below[i - p - 1]
                scaled_below = mine[k] * root
                for j in range(k + 1, SUB):
                    mine[j] = mine[j] - scaled_below * factors[j]
                tiles[i] = tiles[i] - scaled_below * pivot_row
        tiles[p] = rows
    return jnp.concatenate(tiles, axis=0)


def factor_kernel(step, count, v_ref, o_ref):
    here = slice(step * TILE, (step + 1) * TILE)
    o_ref[...] = v_ref[...]
    inverse = factor_tiles([v_ref[step * TILE + i * SUB : step * TILE + (i + 1) * SUB, here] for i in range(TILE // SUB)])
    down = lax.broadcasted_iota(jnp.int32, (TILE, TILE), 0)
    across = lax.broadcasted_iota(jnp.int32, (TILE, TILE), 1)
    inverse = jnp.where(down >= across, inverse, 0.0)
    o_ref[here, :] = jnp.dot(inverse, v_ref[here, :], precision=HI, preferred_element_type=jnp.float32)
    o_ref[here, here] = inverse
    if step + 1 < count:
        below = slice((step + 1) * TILE, count * TILE)
        o_ref[below, here] = jnp.zeros((TILE * (count - step - 1), TILE), jnp.float32)
        o_ref[below, :] = o_ref[below, :] - lax.dot_general(
            o_ref[here, below], o_ref[here, :], (((0,), (0,)), ((), ())), precision=HI, preferred_element_type=jnp.float32
        )


ANYWHERE = pl.BlockSpec(memory_space=pl.ANY)
SCALARS = pl.BlockSpec(memory_space=pltpu.SMEM)
VECTORS = pl.BlockSpec(memory_space=pltpu.VMEM)


def small_kernel(body, name, scalars, values, out_shape, after=(), moved=1):
    def kernel(*refs):
        given = len(scalars) + len(values)
        body(refs[:given], refs[given + len(after) :])

    return pl.pallas_call(
        kernel,
        out_shape=out_shape,
        in_specs=[SCALARS] * len(scalars) + [VECTORS] * len(values) + [ANYWHERE] * len(after),
        compiler_params=pltpu.CompilerParams(vmem_limit_bytes=VMEM_BYTES),
        cost_estimate=pl.CostEstimate(flops=1, bytes_accessed=moved, transcendentals=0),
        name=name,
    )(*scalars, *values, *after)


def f32(*shape):
    return jax.ShapeDtypeStruct(shape, jnp.float32)


def gram_rows(which, block, after=()):
    cells, width = block.shape
    half = width // 2

    def body(given, outs):
        which_ref, x_ref = given
        columns = x_ref[:, pl.ds(pl.multiple_of(which_ref[0] * half, half), half)]
        outs[0][...] = lax.dot_general(
            columns, x_ref[...], (((0,), (0,)), ((), ())), preferred_element_type=jnp.float32
        )

    return small_kernel(body, "gram_rows", [which], [block], f32(half, width), after)


def add_split(order, parts, after=()):
    rows, width = parts[0].shape
    count = order.shape[0]
    share = rows // count

    def body(given, outs):
        order_ref, part_refs = given[0], given[1:]
        for k in range(count):
            place = pl.ds(pl.multiple_of(order_ref[k] * share, share), share)
            total = part_refs[0][place, :]
            for ref in part_refs[1:]:
                total = total + ref[place, :]
            outs[k][...] = total

    return small_kernel(body, "add_split", [order], parts, [f32(share, width)] * count, after)


def add_all(parts, after=()):
    def body(given, outs):
        total = given[0][...]
        for ref in given[1:]:
            total = total + ref[...]
        outs[0][...] = total

    return small_kernel(body, "add_all", [], parts, f32(*parts[0].shape), after)


def place_parts(order, parts, after=()):
    share, width = parts[0].shape
    count = len(parts)

    def body(given, outs):
        for k in range(count):
            outs[0][pl.ds(pl.multiple_of(given[0][k] * share, share), share), :] = given[1 + k][...]

    return small_kernel(body, "place_parts", [order], parts, f32(share * count, width), after)


def copy_rows(value, pieces, after):
    def body(given, outs):
        for (first, count), out in zip(pieces, outs):
            out[...] = given[0][first : first + count, :]

    shapes = [jax.ShapeDtypeStruct((count, value.shape[1]), value.dtype) for _, count in pieces]
    return small_kernel(body, "copy_rows", [], [value], shapes, after)


def live_halves(which, cell_counts, embeddings):
    slots, width = embeddings.shape
    half = slots // 2

    def body(given, outs):
        which_ref, count_ref, x_ref = given
        for out, part in zip(outs, (which_ref[0], 1 - which_ref[0])):
            first = pl.multiple_of(part * half, half)
            row = first + lax.broadcasted_iota(jnp.int32, (half, width), 0)
            values = x_ref[pl.ds(first, half), :]
            out[...] = jnp.where(row < count_ref[0], values.astype(jnp.float32), 0.0).astype(values.dtype)

    shape = jax.ShapeDtypeStruct((half, width), embeddings.dtype)
    return small_kernel(body, "live_halves", [which, cell_counts], [embeddings], [shape] * 2)


def join_features(which, mine, other):
    rows, width = mine.shape

    def body(given, outs):
        which_ref, mine_ref, other_ref = given
        first = which_ref[0] == 0
        values = mine_ref[...], other_ref[...]
        outs[0][:, :width] = jnp.where(first, values[0], values[1])
        outs[0][:, width:] = jnp.where(first, values[1], values[0])

    return small_kernel(
        body, "join_features", [which], [mine, other], jax.ShapeDtypeStruct((rows, 2 * width), mine.dtype)
    )


def choose(which, zero, one, after=()):
    def body(given, outs):
        outs[0][...] = jnp.where(given[0][0] == 1, given[2][...], given[1][...])

    return small_kernel(
        body, "choose", [which], [zero, one], jax.ShapeDtypeStruct(zero.shape, zero.dtype), after
    )


def factor_step(step, value, after=()):
    width = value.shape[0]
    body = lambda given, outs: factor_kernel(step, width // TILE, given[0], outs[0])
    return small_kernel(body, "factor_step", [], [value], f32(width, width), after, moved=FACTOR_BYTES)


def gram_inverse(value, scale, after=()):
    width = value.shape[0]

    def body(given, outs):
        down = lax.broadcasted_iota(jnp.int32, (width, width), 0)
        across = lax.broadcasted_iota(jnp.int32, (width, width), 1)
        lower = jnp.where(down >= across, given[0][...], 0.0)
        outs[0][...] = scale * lax.dot_general(
            lower, lower, (((0,), (0,)), ((), ())), precision=HI, preferred_element_type=jnp.float32
        )

    return small_kernel(body, "gram_inverse", [], [value], f32(width, width), after)


def apply_inverse(inverse, parts):
    width = inverse.shape[0]
    rows = parts[0].shape[0]

    def body(given, outs):
        cross = (given[1][...] + given[2][...]) + (given[3][...] + given[4][...])
        outs[0][...] = lax.dot_general(
            given[0][...], cross, (((1,), (1,)), ((), ())), precision=HI, preferred_element_type=jnp.float32
        )

    return small_kernel(body, "apply_inverse", [], [inverse, *parts], f32(width, rows))


def shards(embeddings, targets_by_gene, cell_counts):
    slots = embeddings.shape[0]
    donors = lax.axis_size("donor")
    donor = lax.axis_index("donor")
    c = lax.axis_index("gene")
    z, y, x = donor // 4, (donor // 2) % 2, donor % 2
    near_bit = jnp.where(c == 0, x, y)
    far_bit = jnp.where(c == 0, y, x)
    half = slots // 2
    ints = lambda *values: jnp.stack(values).astype(jnp.int32)

    def group_donor(k, core, bit):
        line, other = k // 2, k % 2
        return line * 4 + jnp.where(core == 0, other * 2 + bit, bit * 2 + other)

    ks = jnp.arange(8, dtype=jnp.int32)

    def blocks_for(core, bit):
        return (group_donor(ks, core, bit) * 2 + core).astype(jnp.int32)

    core = ints(c)
    keep, give = live_halves(core, cell_counts, embeddings)
    got = send(give, CORE)
    block = join_features(core, keep, got)
    line1 = send(block, LINE[0])
    middle_own = send(block, MIDDLE)
    far_own = send(block, FAR)

    gram_give = gram_rows(ints(1 - c), block)
    gram_got = send(gram_give, CORE)
    gram_keep = gram_rows(ints(c), block, after=(gram_give,))
    mine, give = add_split(ints(near_bit, 1 - near_bit), [gram_keep, gram_got])
    for_core = pick_blocks(targets_by_gene, blocks_for(1 - c, far_bit), half, after=(mine,))
    from_core = send(for_core, CORE)
    mine, give = add_split(ints(far_bit, 1 - far_bit), [mine, send(give, NEAR)], after=(for_core,))
    got = send(give, FAR)
    place = near_bit * 2 + far_bit
    order = ints(place, place ^ jnp.where(c == 0, 2, 1), place ^ jnp.where(c == 0, 1, 2), place ^ 3)

    rows = targets_by_gene.shape[0]
    cut = 6 * rows // 10 // 16 * 16
    near_blocks = blocks_for(c, 1 - near_bit)
    for_near = pick_blocks(targets_by_gene, near_blocks, half, (got, far_own, line1, middle_own), 0, cut)
    near_low = send(for_near, NEAR)
    plane_sum = add_all([mine, got], after=(line1, middle_own))
    line_parts = [plane_sum] + [send(plane_sum, LINE[s]) for s in range(3)]
    total = add_all(line_parts)

    quarters = [total] + [send(total, PLANE[s]) for s in range(3)]
    for_near = pick_blocks(targets_by_gene, near_blocks, half, (total,), cut, rows - cut)
    near_high = send(for_near, NEAR)
    quarter = place_parts(order, quarters, (for_near, near_low, from_core))
    outward_own = send(middle_own, OUTWARD)
    middle_outer = send(line1, MIDDLE)
    for_diag = pick_blocks(targets_by_gene, blocks_for(1 - c, 1 - far_bit), half, (quarter,))
    from_diag = send(for_diag, DIAG_OUT)
    gram = place_parts(ints(c, 1 - c), [quarter, send(quarter, CORE)], after=(for_diag,))

    value = factor_step(0, gram)
    value = factor_step(1, value)
    (late,) = copy_rows(middle_outer, ((0, half),), (value, near_high, outward_own))
    outward_outer = send(late, OUTWARD)
    (late,) = copy_rows(line1, ((0, half),), (late,))
    far1 = send(late, FAR)
    is_middle = jnp.where((z == 1) | (z == 2), 1, 0)
    second = choose(ints(is_middle), outward_own, middle_own, (late,))
    far2 = send(second, FAR)
    value = factor_step(2, value, after=(second,))
    value = factor_step(3, value)
    inverse = gram_inverse(value, math.sqrt(slots * donors))
    second_z = jnp.where(is_middle == 1, z ^ 3, z ^ 2)
    third_z = jnp.where(is_middle == 1, z ^ 2, z ^ 3)

    def cells_of(piece, cells_z, other, part=0):
        k = cells_z * 2 + other
        column = (group_donor(k, c, near_bit) * 2 + c) * (half // piece.shape[0]) + part
        return piece, column, k, part

    received = (from_core, near_low, near_high, from_diag)
    def add(acc, blocks, after=()):
        return cross_add(acc, targets_by_gene, received, [cells_of(*block) for block in blocks], after)

    acc = add(None, [(block, z, far_bit), (far_own, z, 1 - far_bit), (line1, z ^ 1, far_bit)], (inverse,))
    acc = add(acc, [(second, second_z, far_bit), (far1, z ^ 1, 1 - far_bit)])
    third = choose(ints(is_middle), outward_outer, middle_outer, (inverse,))
    far3 = send(third, FAR)
    acc = add(acc, [(third, third_z, far_bit), (far2, second_z, 1 - far_bit)])
    acc = add(acc, [(far3, third_z, 1 - far_bit)])
    own, for_other, to_near, to_diag = acc
    scaled = apply_inverse(
        inverse, [own, send(for_other, CORE), send(to_near, NEAR), send(to_diag, DIAG_BACK)]
    )
    return lax.all_to_all(scaled, "donor", split_axis=0, concat_axis=1, tiled=True)


def solution(mesh):
    placed = (P("donor", "gene"), P(("gene", "donor"), None), P("donor"))
    tuned = mesh.shape["donor"] == 16 and mesh.shape["gene"] == 2
    return jax.shard_map(
        shards if tuned else shards_any_mesh,
        mesh=mesh,
        in_specs=placed,
        out_specs=P("donor", "gene"),
        check_vma=False,
    )
```
